128 devices in a mesh: lon: 32 (over x, z_lo, y), depth: 4 (over z_hi, core).
Axes of the slice: x: 4, y: 4, z: 4 (z_hi: 2, z_lo: 2; z = z_hi * 2 + z_lo), core: 2. Of those that a mesh axis runs over, the one named last changes fastest.
Arguments:
- innovations: float32 [5, 256, 512, 256], P(None, 'depth', 'lon'), may hold values from -6 to 6
- courant: float32 [3, 256, 512, 256], P(None, 'depth', 'lon'), may hold values from -0.3 to 0.3
- diffusivity: float32 [256, 512, 256], P('depth', 'lon'), may hold values from 0.05 to 0.12
- sea_bricks: int32 [256, 32, 128], P('depth', 'lon'), may hold values 0 or 1
- tile_ranks: int32 [32, 8], P('lon'), may hold values from 16 to 128
- row_factors: bfloat16 [32, 8, 4096, 128], P('lon', None, None, 'depth'), may hold values from -0.09375 to 0.09375
- column_factors: bfloat16 [32, 8, 4096, 128], P('lon', None, None, 'depth'), may hold values from -0.25 to 0.25
Outputs:
- initial_adjoint: float32 [256, 512, 256], P('depth', 'lon')
- gradient: float32 [256, 512, 256], P('depth', 'lon')
The draws below stay inside these ranges and needn't reach their ends.
All inputs are finite; a program needn't handle non-finite values. No bound on the sum of `sea_bricks` on one device may be relied on, other than what follows from the above.
Results may differ from the reference program's by a relative error of at most 0.0041.
Values may be sent and summed in bfloat16 or wider, within the bound.
A program may use at most 64 MiB of HBM per device.

```python
import math
import jax
import jax.numpy as jnp
from jax import lax

TILE = 4096
RMAX = 128
NB = 8
STEPS = 4
NY = 256
CX = 16
NX = 512
NZ = 256
N_LON = 32


def set_ends(array, rng, least, largest):
    shape = array.shape
    index_at = [jax.random.randint(jax.random.fold_in(rng, axis), (), 0, shape[axis]) for axis in range(len(shape))]
    array = array.at[tuple(index_at)].set(least)
    longest = shape.index(max(shape))
    index_at[longest] = (index_at[longest] + 1) % shape[longest]
    return array.at[tuple(index_at)].set(largest)


def levels(key, extent, pieces, smallest, high):
    def one(axis_at, shards_of):
        heights = jax.random.uniform(jax.random.fold_in(jax.random.fold_in(key, 6), axis_at), (shards_of,), jnp.float32, smallest / len(pieces), high / len(pieces))
        return jnp.repeat(jnp.exp(heights), extent[axis_at] // shards_of).reshape((-1,) + (1,) * (len(extent) - axis_at - 1))

    loudness = one(*pieces[0])
    for cut in pieces[1:]:
        loudness = loudness * one(*cut)
    return loudness


def scatter_about(rng, dims, deviation, limit, cuts=(), held_as=jnp.bfloat16):
    factor_of = levels(rng, dims, cuts, -0.22, 0.18) if cuts else 1.0
    array = jax.random.normal(rng, dims, jnp.float32) * deviation * factor_of
    return jnp.minimum(jnp.maximum(array, -limit), limit).astype(held_as)


def setup_inputs(seed: int = 0) -> dict:
    streams_of = jax.random.split(jax.random.key(seed), 8)
    return {
        "innovations": scatter_about(streams_of[0], (STEPS + 1, NZ, NX, NY), 1.0, 6.0, ((1, 4), (2, 32)), jnp.float32),
        "courant": jnp.clip(jax.random.uniform(streams_of[1], (3, NZ, NX, NY), jnp.float32, -0.3, 0.3) * levels(streams_of[1], (3, NZ, NX, NY), ((1, 4), (2, 32)), -0.4, 0.0), -0.3, 0.3),
        "diffusivity": jnp.clip(jnp.exp(math.log(0.12) - 0.8754687 * jax.random.uniform(streams_of[2], (NZ, NX, NY), jnp.float32) ** levels(streams_of[2], (NZ, NX, NY), ((0, 4), (1, 32)), -0.2, 0.2)), 0.05, 0.12),
        "sea_bricks": set_ends((jax.random.randint(streams_of[3], (NZ, N_LON, NY // 2), 0, 4) < 3).astype(jnp.int32), jax.random.fold_in(streams_of[3], 1), 0, 1),
        "tile_ranks": set_ends(jax.random.randint(streams_of[4], (N_LON, NB), 16, 129), jax.random.fold_in(streams_of[4], 1), 16, 128).astype(jnp.int32),
        "row_factors": scatter_about(streams_of[5], (N_LON, NB, TILE, RMAX), TILE ** -0.5, 0.09375, ((0, 32), (3, 4))),
        "column_factors": scatter_about(streams_of[6], (N_LON, NB, TILE, RMAX), (RMAX * NB // 2) ** -0.5, 0.25, ((0, 32), (3, 4))),
    }


def lat_terms(plus_term, minus_term):
    lower = jnp.pad(plus_term[:, :, :-1], ((0, 0), (0, 0), (1, 0)))
    upper = jnp.pad(minus_term[:, :, 1:], ((0, 0), (0, 0), (0, 1)))
    return lower + upper


def adjoint_apply(lam, plus, minus, center):
    plus_term = plus * lam
    minus_term = minus * lam
    out = center * lam
    out = out + jnp.pad(plus_term[0][:-1], ((1, 0), (0, 0), (0, 0)))
    out = out + jnp.pad(minus_term[0][1:], ((0, 1), (0, 0), (0, 0)))
    out = out + jnp.roll(plus_term[1], 1, axis=1) + jnp.roll(minus_term[1], -1, axis=1)
    return out + lat_terms(plus_term[2], minus_term[2])


def row_coeffs(args):
    block, factors, ranks = args
    coeff = jnp.einsum('zt,ktr->kzr', block.astype(jnp.float32), factors.astype(jnp.float32))
    columns = jnp.arange(RMAX, dtype=jnp.int32)
    keep = (columns[None, :] < ranks[:, None]).astype(jnp.float32)
    return (coeff * keep[:, None, :]).astype(jnp.bfloat16)


def column_sum(args):
    received, factors = args
    return jnp.einsum('kzr,ktr->zt', received.astype(jnp.float32), factors.astype(jnp.float32))


def reference(innovations, courant, diffusivity, sea_bricks, tile_ranks, row_factors, column_factors):
    sea = sea_bricks.astype(jnp.float32)
    sea = jnp.broadcast_to(sea[:, :, None, :, None], (NZ, N_LON, CX, NY // 2, 2)).reshape(NZ, NX, NY)
    plus = diffusivity[None] - 0.5 * courant
    minus = diffusivity[None] + 0.5 * courant
    center = 1.0 - 6.0 * diffusivity
    lam = sea * innovations[STEPS]
    for step in reversed(range(STEPS)):
        lam = sea * (adjoint_apply(lam, plus, minus, center) + innovations[step])
    blocks = lam.astype(jnp.bfloat16).reshape(NZ, N_LON, TILE).transpose(1, 0, 2)
    coeff = lax.map(row_coeffs, (blocks, row_factors, tile_ranks))
    received = jnp.stack([jnp.roll(coeff[:, k], k - NB // 2, axis=0) for k in range(NB)], axis=1)
    sums = lax.map(column_sum, (received, column_factors))
    gradient = sums.transpose(1, 0, 2).reshape(NZ, NX, NY)
    return lam, gradient
```

```python
import functools

import jax
import jax.numpy as jnp
from jax import lax
from jax.experimental import pallas as pl
from jax.experimental.pallas import tpu as pltpu
from jax.sharding import PartitionSpec as P

MESH = pl.DeviceIdType.MESH
F32, BF16 = jnp.float32, jnp.bfloat16
NT = (((1,), (1,)), ((), ()))
CHUNKS = 4
EARLY = (1, 2)
LATE = (0, 3)
ORDER = (1, 2, 0, 3)


def kernel(
    peers, inn_h, cou_h, dif_h, sea_h, ranks, u_h, v_h, lam_o, grad_o,
    inn, cou, dif, brick, sea, coef_x, coef_z, u, v, fx, fz, rx, rz,
    blk, rblk, cs_own, cs, cr_own, cr, g_own, gs, gr, out,
    load, face_s, face_r, rank_s, rank_r, blk_s, blk_r, co_s, co_r, g_s, g_r, done,
):
    levels, lons, lats = dif.shape
    slots, ranks_here = u_h.shape[0], u_h.shape[1]
    steps = inn.shape[0] - 1
    lv = levels // CHUNKS
    lon, depth = lax.axis_index("lon"), lax.axis_index("depth")
    partner = depth + 1 - 2 * lax.rem(depth, 2)
    peer = lax.rem(depth + 2, 4)

    def lon_at(shift):
        return (lax.rem(lon + shift + peers, peers), depth)

    def send(src, dst, ssem, rsem, to):
        return pltpu.make_async_remote_copy(
            src_ref=src, dst_ref=dst, send_sem=ssem, recv_sem=rsem, device_id=to, device_id_type=MESH
        )

    barrier = pltpu.get_barrier_semaphore()
    friends = [lon_at(s) for s in range(-4, 5) if s != 0] + [(lon, lax.rem(depth + i, 4)) for i in (1, 2, 3)]
    for to in friends:
        pl.semaphore_signal(barrier, inc=1, device_id=to, device_id_type=MESH)

    def fetch(src, dst, i):
        copy = pltpu.make_async_copy(src, dst, load.at[i])
        copy.start()
        return copy

    first = [
        fetch(sea_h, brick, 0),
        fetch(inn_h.at[4], inn.at[4], 1),
        fetch(dif_h, dif, 2),
        fetch(cou_h.at[1], cou.at[1], 3),
        fetch(cou_h.at[0], cou.at[0], 4),
    ]
    second = [
        fetch(inn_h.at[3], inn.at[3], 5),
        fetch(cou_h.at[2], cou.at[2], 6),
    ]
    third = [fetch(inn_h.at[k], inn.at[k], 7 + k) for k in (2, 1, 0)]
    u_own = fetch(u_h, u.at[:, 0:ranks_here], 10)
    v_own = fetch(v_h, v.at[:, 0:ranks_here], 11)

    half = slots // 2
    rank_copies = []
    for i, (src, dst) in enumerate(((u_h, u), (u_h, u), (v_h, v), (v_h, v))):
        ks = pl.ds((i % 2) * half, half)
        rank_copies.append(
            send(
                src.at[ks], dst.at[ks, ranks_here : 2 * ranks_here],
                rank_s.at[i], rank_r.at[i], (lon, partner),
            )
        )

    for c in first:
        c.wait()
    bricks = lats // 2
    spread = lax.broadcasted_iota(jnp.int32, (bricks, lats), 1) // 2 == lax.broadcasted_iota(
        jnp.int32, (bricks, lats), 0
    )
    sea[...] = jnp.dot(
        brick[...].astype(F32).astype(BF16), spread.astype(F32).astype(BF16), preferred_element_type=F32
    )
    east = lons - 1
    coef_x[0] = dif[:, east, :] - 0.5 * cou[1, :, east, :]
    coef_x[1] = dif[:, 0, :] + 0.5 * cou[1, :, 0, :]
    coef_z[0] = dif[levels - 1] - 0.5 * cou[0, levels - 1]
    coef_z[1] = dif[0] + 0.5 * cou[0, 0]

    for x in (0, east):
        inn[4, :, x, :] = inn[4, :, x, :] * sea[...]
    for z in (0, levels - 1):
        mask = jnp.broadcast_to(sea[z : z + 1], (lons, lats))
        inn[4, z, 1:east] = (inn[4, z] * mask)[1:east]

    def x_faces(n):
        return [
            send(fx.at[n, i], rx.at[n, i], face_s.at[n, i], face_r.at[n, i], lon_at(1 - 2 * i))
            for i in range(2)
        ]

    def z_faces(n):
        return [
            send(
                fz.at[n, i], rz.at[n, i], face_s.at[n, 2 + i], face_r.at[n, 2 + i],
                (lon, lax.rem(depth + 5 - 2 * i, 4)),
            )
            for i in range(2)
        ]

    sends_up, sends_down = depth < 3, depth > 0

    def start_faces(n, k):
        up, down = z_faces(n)
        to_east, to_west = x_faces(n)
        fx[n, 0] = (coef_x[0] * inn[k, :, east, :]).astype(BF16)
        to_east.start()
        fx[n, 1] = (coef_x[1] * inn[k, :, 0, :]).astype(BF16)
        to_west.start()
        fz[n, 0] = coef_z[0] * inn[k, levels - 1]
        fz[n, 1] = coef_z[1] * inn[k, 0]

        @pl.when(sends_up)
        def _():
            up.start()

        @pl.when(sends_down)
        def _():
            down.start()

    def add_faces(n, k):
        up, down = z_faces(n)
        to_east, to_west = x_faces(n)
        to_east.wait_recv()
        inn[k, :, 0, :] = inn[k, :, 0, :] + sea[...] * rx[n, 0].astype(F32)
        to_west.wait_recv()
        inn[k, :, east, :] = inn[k, :, east, :] + sea[...] * rx[n, 1].astype(F32)

        @pl.when(sends_down)
        def _():
            up.wait_recv()
            inn[k, 0] = inn[k, 0] + jnp.broadcast_to(sea[0:1], (lons, lats)) * rz[n, 0]

        @pl.when(sends_up)
        def _():
            down.wait_recv()
            z = levels - 1
            inn[k, z] = inn[k, z] + jnp.broadcast_to(sea[z : z + 1], (lons, lats)) * rz[n, 1]

    row = lax.broadcasted_iota(jnp.int32, (lons, lats), 0)
    lane = lax.broadcasted_iota(jnp.int32, (lons, lats), 1)

    def sweep(k):
        def level(z, lower):
            a = inn[k + 1, z]
            half_a = 0.5 * a
            da = dif[z] * a
            c0, c1, c2 = (cou[i, z] * half_a for i in range(3))
            t = inn[k, z] + (a - 6.0 * da) + lower
            t = t + jnp.where(row == 0, 0.0, pltpu.roll(da - c1, 1, 0))
            t = t + jnp.where(row == lons - 1, 0.0, pltpu.roll(da + c1, lons - 1, 0))
            t = t + jnp.where(lane == 0, 0.0, pltpu.roll(da - c2, 1, 1))
            t = t + jnp.where(lane == lats - 1, 0.0, pltpu.roll(da + c2, lats - 1, 1))
            return t, da - c0, da + c0

        def masked(z):
            return jnp.broadcast_to(sea[pl.ds(z, 1)], (lons, lats))

        def body(z, carry):
            t, p = carry
            t_new, p_new, m = level(z, p)
            inn[k, z - 1] = masked(z - 1) * (t + m)
            return t_new, p_new

        t, p, _ = level(0, jnp.zeros((lons, lats), F32))
        t, _ = lax.fori_loop(1, levels, body, (t, p), unroll=3)
        inn[k, levels - 1] = masked(levels - 1) * t

    pl.semaphore_wait(barrier, len(friends))
    start_faces(0, 4)
    rank_copies[0].start()

    def mask_level(z, _):
        inn[4, z, 1:east] = (inn[4, z] * jnp.broadcast_to(sea[pl.ds(z, 1)], (lons, lats)))[1:east]
        return 0

    lax.fori_loop(1, levels - 1, mask_level, 0, unroll=2)
    for c in second:
        c.wait()

    def block_piece(c, x):
        blk[c, x] = inn[0, c * lv : (c + 1) * lv, x, :].astype(BF16)

    def block_send(c, i):
        at = {0: pl.ds(1, lons - 2), 1: pl.ds(0, 1), 2: pl.ds(lons - 1, 1), 3: pl.ds(0, lons)}[i]
        return send(blk.at[c, at], rblk.at[c, at], blk_s.at[c, i], blk_r.at[c, i], (lon, peer))

    for n in range(steps):
        k = steps - 1 - n
        if n > 0:
            third[n - 1].wait()
        sweep(k)
        if n == steps - 1:
            for c in EARLY:
                for x in range(1, east):
                    block_piece(c, x)
                block_send(c, 0).start()
        add_faces(n, k)
        if n < steps - 1:
            start_faces(n + 1, k)
            rank_copies[n + 1].start()

    lam_copy = pltpu.make_async_copy(inn.at[0], lam_o, done.at[0])
    lam_copy.start()
    for c in EARLY:
        for i, x in ((1, 0), (2, east)):
            block_piece(c, x)
            block_send(c, i).start()
    for c in LATE:
        for x in range(lons):
            block_piece(c, x)
        block_send(c, 3).start()

    width = 2 * ranks_here
    col = lax.broadcasted_iota(jnp.int32, (1, slots * width), 1)
    slot, r = col // width, lax.rem(col, width)
    rank = jnp.where(r < ranks_here, depth * ranks_here + r, partner * ranks_here + r - ranks_here)
    limit = jnp.zeros_like(col)
    for s in range(slots):
        limit = jnp.where(slot == s, ranks[0, s], limit)
    keep = (rank < limit).astype(F32)
    tiles = slots // 2
    tile = 2 * width

    def coefficients(lhs, rows, dst):
        acc = jnp.zeros((rows, slots * width), F32)
        for x in range(lons):
            right = u[:, :, x * lats : (x + 1) * lats].reshape(slots * width, lats)
            acc = acc + lax.dot_general(lhs(x), right, NT, preferred_element_type=F32)
        acc = (acc * keep).astype(BF16)
        for i in range(tiles):
            dst[i] = acc[:, i * tile : (i + 1) * tile]

    def shifts(src, dst, b):
        return {
            s: send(src.at[s // 2], dst.at[s], co_s.at[b, s], co_r.at[b, s], lon_at(s - slots // 2))
            for s in range(slots)
            if s != slots // 2
        }

    def received(src, dst, rows):
        low = lax.broadcasted_iota(jnp.int32, (rows, tile), 1) < width
        home = slots // 2
        get = lambda s: src[s // 2] if s == home else dst[s]
        return [jnp.where(low, get(2 * i), get(2 * i + 1)) for i in range(tiles)]

    def sums(parts, x):
        total = None
        for i, part in enumerate(parts):
            right = v[2 * i : 2 * i + 2, :, x * lats : (x + 1) * lats].reshape(tile, lats)
            term = jnp.dot(part, right, preferred_element_type=F32)
            total = term if total is None else total + term
        return total

    own_shifts = shifts(cs_own, cr_own, CHUNKS)
    chunk_shifts = [shifts(cs.at[c], cr.at[c], c) for c in range(CHUNKS)]

    u_own.wait()
    rank_copies[0].wait_recv()
    rank_copies[1].wait_recv()
    coefficients(lambda x: blk[:, x].reshape(levels, lats), levels, cs_own)
    for c in own_shifts.values():
        c.start()

    def chunk_coefficients(c):
        for i in ((0, 1, 2) if c in EARLY else (3,)):
            block_send(c, i).wait_recv()
        coefficients(lambda x: rblk[c, x], lv, cs.at[c])
        for copy in chunk_shifts[c].values():
            copy.start()

    group = lons // 4

    def sum_send(c, i):
        at = pl.ds(i * group, group)
        return send(gs.at[c, at], gr.at[c, at], g_s.at[c, i], g_r.at[c, i], (lon, peer))

    def own_sums():
        for copy in own_shifts.values():
            copy.wait_recv()
        parts = received(cs_own, cr_own, levels)
        for x in range(lons):
            g_own[x] = sums(parts, x)

    def chunk_sums(c):
        for copy in chunk_shifts[c].values():
            copy.wait_recv()
        parts = received(cs.at[c], cr.at[c], lv)
        for i in range(4):
            for x in range(i * group, (i + 1) * group):
                gs[c, x] = sums(parts, x).astype(BF16)
            sum_send(c, i).start()

    chunk_coefficients(ORDER[0])
    v_own.wait()
    rank_copies[2].wait_recv()
    rank_copies[3].wait_recv()
    own_sums()
    chunk_coefficients(ORDER[1])
    for n in range(2, CHUNKS):
        chunk_coefficients(ORDER[n])
        chunk_sums(ORDER[n - 2])
    chunk_sums(ORDER[CHUNKS - 2])
    chunk_sums(ORDER[CHUNKS - 1])

    results = []
    for c in ORDER:
        at = pl.ds(c * lv, lv)
        for i in range(4):
            sum_send(c, i).wait_recv()
            for x in range(i * group, (i + 1) * group):
                out[at, x, :] = g_own[x, at, :] + gr[c, x].astype(F32)
        copy = pltpu.make_async_copy(out.at[at], grad_o.at[at], done.at[1 + c])
        copy.start()
        results.append(copy)

    for n in range(steps):
        up, down = z_faces(n)
        for copy in x_faces(n):
            copy.wait_send()

        @pl.when(sends_up)
        def _():
            up.wait_send()

        @pl.when(sends_down)
        def _():
            down.wait_send()

    for copy in rank_copies:
        copy.wait_send()
    for c in range(CHUNKS):
        for i in ((0, 1, 2) if c in EARLY else (3,)):
            block_send(c, i).wait_send()
        for i in range(4):
            sum_send(c, i).wait_send()
        for copy in chunk_shifts[c].values():
            copy.wait_send()
    for copy in own_shifts.values():
        copy.wait_send()
    lam_copy.wait()
    for copy in results:
        copy.wait()


def per_device(
    peers, innovations, courant, diffusivity, sea_bricks, tile_ranks, row_factors, column_factors
):
    levels, lons, lats = diffusivity.shape
    slots, cols, here = row_factors.shape[1:]
    steps = innovations.shape[0] - 1
    lv = levels // CHUNKS
    dma = pltpu.SemaphoreType.DMA
    anywhere = pl.BlockSpec(memory_space=pl.ANY)
    field = jax.ShapeDtypeStruct(diffusivity.shape, F32)
    lam, gradient = pl.pallas_call(
        functools.partial(kernel, peers),
        out_shape=(field, field),
        in_specs=[anywhere] * 4 + [pl.BlockSpec(memory_space=pltpu.SMEM)] + [anywhere] * 2,
        out_specs=(anywhere, anywhere),
        scratch_shapes=[
            pltpu.VMEM(innovations.shape, F32),
            pltpu.VMEM(courant.shape, F32),
            pltpu.VMEM(diffusivity.shape, F32),
            pltpu.VMEM((levels, lats // 2), jnp.int32),
            pltpu.VMEM((levels, lats), F32),
            pltpu.VMEM((2, levels, lats), F32),
            pltpu.VMEM((2, lons, lats), F32),
            pltpu.VMEM((slots, 2 * here, cols), BF16),
            pltpu.VMEM((slots, 2 * here, cols), BF16),
            pltpu.VMEM((steps, 2, levels, lats), BF16),
            pltpu.VMEM((steps, 2, lons, lats), F32),
            pltpu.VMEM((steps, 2, levels, lats), BF16),
            pltpu.VMEM((steps, 2, lons, lats), F32),
            pltpu.VMEM((CHUNKS, lons, lv, lats), BF16),
            pltpu.VMEM((CHUNKS, lons, lv, lats), BF16),
            pltpu.VMEM((slots // 2, levels, 4 * here), BF16),
            pltpu.VMEM((CHUNKS, slots // 2, lv, 4 * here), BF16),
            pltpu.VMEM((slots, levels, 4 * here), BF16),
            pltpu.VMEM((CHUNKS, slots, lv, 4 * here), BF16),
            pltpu.VMEM((lons, levels, lats), F32),
            pltpu.VMEM((CHUNKS, lons, lv, lats), BF16),
            pltpu.VMEM((CHUNKS, lons, lv, lats), BF16),
            pltpu.VMEM(diffusivity.shape, F32),
            dma((12,)),
            dma((steps, 4)),
            dma((steps, 4)),
            dma((4,)),
            dma((4,)),
            dma((CHUNKS, 4)),
            dma((CHUNKS, 4)),
            dma((CHUNKS + 1, slots)),
            dma((CHUNKS + 1, slots)),
            dma((CHUNKS, 4)),
            dma((CHUNKS, 4)),
            dma((1 + CHUNKS,)),
        ],
        compiler_params=pltpu.CompilerParams(collective_id=0, has_side_effects=True),
    )(
        innovations,
        courant,
        diffusivity,
        sea_bricks.reshape(levels, lats // 2),
        tile_ranks,
        jnp.swapaxes(row_factors[0], 1, 2),
        jnp.swapaxes(column_factors[0], 1, 2),
    )
    return lam, gradient


def solution(mesh):
    placed = (
        P(None, "depth", "lon", None),
        P(None, "depth", "lon", None),
        P("depth", "lon", None),
        P("depth", "lon", None),
        P("lon", None),
        P("lon", None, None, "depth"),
        P("lon", None, None, "depth"),
    )
    return jax.shard_map(
        functools.partial(per_device, mesh.shape["lon"]),
        mesh=mesh,
        in_specs=placed,
        out_specs=(P("depth", "lon", None), P("depth", "lon", None)),
        check_vma=False,
    )
```

```python
import functools

import jax
import jax.numpy as jnp
from jax import lax
from jax.experimental import pallas as pl
from jax.experimental.pallas import tpu as pltpu
from jax.sharding import PartitionSpec as P

MESH = pl.DeviceIdType.MESH
F32, BF16 = jnp.float32, jnp.bfloat16
NT = (((1,), (1,)), ((), ()))
CHUNKS = 4
ORDER = (1, 2, 0, 3)
GROUPS = ((0, 1), (1, 3), (3, 4))


def kernel(
    peers, inn_h, cou_h, dif_h, sea_h, ranks, u_h, v_h, lam_o, grad_o,
    inn, cou, dif, brick, sea, coef_x, coef_z, u, v, fx, fz, rx, rz,
    blk, rblk, cs_own, cs, cr_own, cr, g_own, gs, gr,
    load, face_s, face_r, rank_s, rank_r, blk_s, blk_r, co_s, co_r, g_s, g_r,
):
    levels, lons, lats = dif.shape
    slots, ranks_here = u_h.shape[0], u_h.shape[1]
    steps = inn.shape[0] - 1
    lv = levels // CHUNKS
    lon, depth = lax.axis_index("lon"), lax.axis_index("depth")
    partner = depth + 1 - 2 * lax.rem(depth, 2)
    peer = lax.rem(depth + 2, 4)

    def lon_at(shift):
        return (lax.rem(lon + shift + peers, peers), depth)

    def send(src, dst, ssem, rsem, to):
        return pltpu.make_async_remote_copy(
            src_ref=src, dst_ref=dst, send_sem=ssem, recv_sem=rsem, device_id=to, device_id_type=MESH
        )

    barrier = pltpu.get_barrier_semaphore()
    friends = [lon_at(s) for s in range(-4, 5) if s != 0] + [(lon, lax.rem(depth + i, 4)) for i in (1, 2, 3)]
    for to in friends:
        pl.semaphore_signal(barrier, inc=1, device_id=to, device_id_type=MESH)

    def fetch(src, dst, i):
        copy = pltpu.make_async_copy(src, dst, load.at[i])
        copy.start()
        return copy

    first = [
        fetch(sea_h, brick, 0),
        fetch(inn_h.at[4], inn.at[4], 1),
        fetch(dif_h, dif, 2),
        fetch(cou_h.at[1], cou.at[1], 3),
        fetch(cou_h.at[0], cou.at[0], 4),
    ]
    second = [
        fetch(inn_h.at[3], inn.at[3], 5),
        fetch(cou_h.at[2], cou.at[2], 6),
    ]
    third = [fetch(inn_h.at[k], inn.at[k], 7 + k) for k in (2, 1, 0)]
    u_own = fetch(u_h, u.at[:, 0:ranks_here], 10)
    v_own = fetch(v_h, v.at[:, 0:ranks_here], 11)

    half = slots // 2
    rank_copies = []
    for i, (src, dst) in enumerate(((u_h, u), (u_h, u), (v_h, v), (v_h, v))):
        ks = pl.ds((i % 2) * half, half)
        rank_copies.append(
            send(
                src.at[ks], dst.at[ks, ranks_here : 2 * ranks_here],
                rank_s.at[i], rank_r.at[i], (lon, partner),
            )
        )

    for c in first:
        c.wait()
    bricks = lats // 2
    spread = lax.broadcasted_iota(jnp.int32, (bricks, lats), 1) // 2 == lax.broadcasted_iota(
        jnp.int32, (bricks, lats), 0
    )
    sea[...] = jnp.dot(
        brick[...].astype(F32).astype(BF16), spread.astype(F32).astype(BF16), preferred_element_type=F32
    )
    east = lons - 1
    coef_x[0] = dif[:, east, :] - 0.5 * cou[1, :, east, :]
    coef_x[1] = dif[:, 0, :] + 0.5 * cou[1, :, 0, :]
    coef_z[0] = dif[levels - 1] - 0.5 * cou[0, levels - 1]
    coef_z[1] = dif[0] + 0.5 * cou[0, 0]

    for x in (0, east):
        inn[4, :, x, :] = inn[4, :, x, :] * sea[...]
    for z in (0, levels - 1):
        mask = jnp.broadcast_to(sea[z : z + 1], (lons, lats))
        inn[4, z, 1:east] = (inn[4, z] * mask)[1:east]

    def x_faces(n):
        return [
            send(fx.at[n, i], rx.at[n, i], face_s.at[n, i], face_r.at[n, i], lon_at(1 - 2 * i))
            for i in range(2)
        ]

    def z_faces(n):
        return [
            send(
                fz.at[n, i], rz.at[n, i], face_s.at[n, 2 + i], face_r.at[n, 2 + i],
                (lon, lax.rem(depth + 5 - 2 * i, 4)),
            )
            for i in range(2)
        ]

    sends_up, sends_down = depth < 3, depth > 0

    def start_faces(n, k):
        up, down = z_faces(n)
        to_east, to_west = x_faces(n)
        fx[n, 0] = (coef_x[0] * inn[k, :, east, :]).astype(BF16)
        to_east.start()
        fx[n, 1] = (coef_x[1] * inn[k, :, 0, :]).astype(BF16)
        to_west.start()
        fz[n, 0] = coef_z[0] * inn[k, levels - 1]
        fz[n, 1] = coef_z[1] * inn[k, 0]

        @pl.when(sends_up)
        def _():
            up.start()

        @pl.when(sends_down)
        def _():
            down.start()

    def add_faces(n, k):
        up, down = z_faces(n)
        to_east, to_west = x_faces(n)
        to_east.wait_recv()
        inn[k, :, 0, :] = inn[k, :, 0, :] + sea[...] * rx[n, 0].astype(F32)
        to_west.wait_recv()
        inn[k, :, east, :] = inn[k, :, east, :] + sea[...] * rx[n, 1].astype(F32)

        @pl.when(sends_down)
        def _():
            up.wait_recv()
            inn[k, 0] = inn[k, 0] + jnp.broadcast_to(sea[0:1], (lons, lats)) * rz[n, 0]

        @pl.when(sends_up)
        def _():
            down.wait_recv()
            z = levels - 1
            inn[k, z] = inn[k, z] + jnp.broadcast_to(sea[z : z + 1], (lons, lats)) * rz[n, 1]

    row = lax.broadcasted_iota(jnp.int32, (lons, lats), 0)
    lane = lax.broadcasted_iota(jnp.int32, (lons, lats), 1)

    def sweep(k):
        def level(z, lower):
            a = inn[k + 1, z]
            half_a = 0.5 * a
            da = dif[z] * a
            c0, c1, c2 = (cou[i, z] * half_a for i in range(3))
            t = inn[k, z] + (a - 6.0 * da) + lower
            t = t + jnp.where(row == 0, 0.0, pltpu.roll(da - c1, 1, 0))
            t = t + jnp.where(row == lons - 1, 0.0, pltpu.roll(da + c1, lons - 1, 0))
            t = t + jnp.where(lane == 0, 0.0, pltpu.roll(da - c2, 1, 1))
            t = t + jnp.where(lane == lats - 1, 0.0, pltpu.roll(da + c2, lats - 1, 1))
            return t, da - c0, da + c0

        def masked(z):
            return jnp.broadcast_to(sea[pl.ds(z, 1)], (lons, lats))

        def body(z, carry):
            t, p = carry
            t_new, p_new, m = level(z, p)
            inn[k, z - 1] = masked(z - 1) * (t + m)
            return t_new, p_new

        t, p, _ = level(0, jnp.zeros((lons, lats), F32))
        t, _ = lax.fori_loop(1, levels, body, (t, p), unroll=9)
        inn[k, levels - 1] = masked(levels - 1) * t

    pl.semaphore_wait(barrier, len(friends))
    start_faces(0, 4)
    rank_copies[0].start()

    def mask_level(z, _):
        inn[4, z, 1:east] = (inn[4, z] * jnp.broadcast_to(sea[pl.ds(z, 1)], (lons, lats)))[1:east]
        return 0

    lax.fori_loop(1, levels - 1, mask_level, 0, unroll=2)
    for c in second:
        c.wait()

    def block_piece(p, x):
        z = ORDER[p] * lv
        blk[p, x] = inn[0, z : z + lv, x, :].astype(BF16)

    def block_send(p, i):
        at = (pl.ds(1, lons - 2), pl.ds(0, 1), pl.ds(lons - 1, 1), pl.ds(0, lons))[i]
        return send(blk.at[p, at], rblk.at[p, at], blk_s.at[p, i], blk_r.at[p, i], (lon, peer))

    pieces = [[block_send(p, i) for i in ((0, 1, 2) if p == 0 else (3,))] for p in range(CHUNKS)]

    for n in range(steps):
        k = steps - 1 - n
        if n > 0:
            third[n - 1].wait()
        sweep(k)
        if n == steps - 1:
            for x in range(1, east):
                block_piece(0, x)
            pieces[0][0].start()
            for x in range(1, east):
                block_piece(1, x)
        add_faces(n, k)
        if n < steps - 1:
            start_faces(n + 1, k)
            rank_copies[n + 1].start()

    for x in (0, east):
        block_piece(0, x)
    pieces[0][1].start()
    pieces[0][2].start()
    for x in (0, east):
        block_piece(1, x)
    pieces[1][0].start()
    for p in (2, 3):
        for x in range(lons):
            block_piece(p, x)
        pieces[p][0].start()

    width = 2 * ranks_here
    col = lax.broadcasted_iota(jnp.int32, (1, slots * width), 1)
    slot, r = col // width, lax.rem(col, width)
    rank = jnp.where(r < ranks_here, depth * ranks_here + r, partner * ranks_here + r - ranks_here)
    limit = jnp.zeros_like(col)
    for s in range(slots):
        limit = jnp.where(slot == s, ranks[0, s], limit)
    keep = (rank < limit).astype(F32)
    tiles = slots // 2
    tile = 2 * width

    home = slots // 2

    def coefficients(src, first_p, last_p, dst):
        rows = (last_p - first_p) * lv
        acc = jnp.zeros((rows, slots * width), F32)
        for x in range(lons):
            left = src[first_p:last_p, x].reshape(rows, lats)
            right = u[:, :, x * lats : (x + 1) * lats].reshape(slots * width, lats)
            acc = acc + lax.dot_general(left, right, NT, preferred_element_type=F32)
        acc = (acc * keep).astype(BF16)
        for i in range(tiles):
            dst[i, first_p * lv : last_p * lv] = acc[:, i * tile : (i + 1) * tile]

    def shifts(src, dst, b, first_p, last_p):
        at = pl.ds(first_p * lv, (last_p - first_p) * lv)
        return [
            send(src.at[s // 2, at], dst.at[s, at], co_s.at[b, s], co_r.at[b, s], lon_at(s - home))
            for s in range(slots)
            if s != home
        ]

    def received(src, dst, first_p, last_p):
        at = slice(first_p * lv, last_p * lv)
        low = lax.broadcasted_iota(jnp.int32, ((last_p - first_p) * lv, tile), 1) < width
        get = lambda s: src[s // 2, at] if s == home else dst[s, at]
        return [jnp.where(low, get(2 * i), get(2 * i + 1)) for i in range(tiles)]

    def sums(parts, x):
        total = None
        for i, part in enumerate(parts):
            right = v[2 * i : 2 * i + 2, :, x * lats : (x + 1) * lats].reshape(tile, lats)
            term = jnp.dot(part, right, preferred_element_type=F32)
            total = term if total is None else total + term
        return total

    own_shifts = shifts(cs_own, cr_own, len(GROUPS), 0, CHUNKS)
    group_shifts = [shifts(cs, cr, g, *GROUPS[g]) for g in range(len(GROUPS))]
    part = lons // 4

    def sum_send(g, i):
        first_p, last_p = GROUPS[g]
        at = (pl.ds(i * part, part), pl.ds(first_p * lv, (last_p - first_p) * lv))
        return send(gs.at[at], gr.at[at], g_s.at[g, i], g_r.at[g, i], (lon, peer))

    sum_sends = [[sum_send(g, i) for i in range(4)] for g in range(len(GROUPS))]

    def group_coefficients(g):
        for p in range(*GROUPS[g]):
            for copy in pieces[p]:
                copy.wait_recv()
        coefficients(rblk, *GROUPS[g], cs)
        for copy in group_shifts[g]:
            copy.start()

    def group_sums(g):
        first_p, last_p = GROUPS[g]
        for copy in group_shifts[g]:
            copy.wait_recv()
        parts = received(cs, cr, first_p, last_p)
        for i in range(4):
            for x in range(i * part, (i + 1) * part):
                gs[x, first_p * lv : last_p * lv] = sums(parts, x).astype(BF16)
            sum_sends[g][i].start()

    u_own.wait()
    rank_copies[0].wait_recv()
    rank_copies[1].wait_recv()
    coefficients(blk, 0, CHUNKS, cs_own)
    for copy in own_shifts:
        copy.start()
    lam_o[...] = inn[0]
    group_coefficients(0)
    group_coefficients(1)
    v_own.wait()
    rank_copies[2].wait_recv()
    rank_copies[3].wait_recv()
    group_sums(0)
    group_coefficients(2)
    group_sums(1)
    group_sums(2)
    for copy in own_shifts:
        copy.wait_recv()
    parts = received(cs_own, cr_own, 0, CHUNKS)
    for x in range(lons):
        g_own[x] = sums(parts, x)

    for g, (first_p, last_p) in enumerate(GROUPS):
        for i in range(4):
            sum_sends[g][i].wait_recv()
            for x in range(i * part, (i + 1) * part):
                for p in range(first_p, last_p):
                    at, z = slice(p * lv, (p + 1) * lv), ORDER[p] * lv
                    grad_o[z : z + lv, x, :] = g_own[x, at, :] + gr[x, at].astype(F32)

    for n in range(steps):
        up, down = z_faces(n)
        for copy in x_faces(n):
            copy.wait_send()

        @pl.when(sends_up)
        def _():
            up.wait_send()

        @pl.when(sends_down)
        def _():
            down.wait_send()

    for copy in rank_copies:
        copy.wait_send()
    for copies in pieces + sum_sends + group_shifts + [own_shifts]:
        for copy in copies:
            copy.wait_send()


def per_device(
    peers, innovations, courant, diffusivity, sea_bricks, tile_ranks, row_factors, column_factors
):
    levels, lons, lats = diffusivity.shape
    slots, cols, here = row_factors.shape[1:]
    steps = innovations.shape[0] - 1
    lv = levels // CHUNKS
    dma = pltpu.SemaphoreType.DMA
    anywhere = pl.BlockSpec(memory_space=pl.ANY)
    lam, gradient = pl.pallas_call(
        functools.partial(kernel, peers),
        out_shape=(pltpu.VMEM(diffusivity.shape, F32),) * 2,
        in_specs=[anywhere] * 4 + [pl.BlockSpec(memory_space=pltpu.SMEM)] + [anywhere] * 2,
        out_specs=(pl.BlockSpec(memory_space=pltpu.VMEM),) * 2,
        scratch_shapes=[
            pltpu.VMEM(innovations.shape, F32),
            pltpu.VMEM(courant.shape, F32),
            pltpu.VMEM(diffusivity.shape, F32),
            pltpu.VMEM((levels, lats // 2), jnp.int32),
            pltpu.VMEM((levels, lats), F32),
            pltpu.VMEM((2, levels, lats), F32),
            pltpu.VMEM((2, lons, lats), F32),
            pltpu.VMEM((slots, 2 * here, cols), BF16),
            pltpu.VMEM((slots, 2 * here, cols), BF16),
            pltpu.VMEM((steps, 2, levels, lats), BF16),
            pltpu.VMEM((steps, 2, lons, lats), F32),
            pltpu.VMEM((steps, 2, levels, lats), BF16),
            pltpu.VMEM((steps, 2, lons, lats), F32),
            pltpu.VMEM((CHUNKS, lons, lv, lats), BF16),
            pltpu.VMEM((CHUNKS, lons, lv, lats), BF16),
            pltpu.VMEM((slots // 2, levels, 4 * here), BF16),
            pltpu.VMEM((slots // 2, levels, 4 * here), BF16),
            pltpu.VMEM((slots, levels, 4 * here), BF16),
            pltpu.VMEM((slots, levels, 4 * here), BF16),
            pltpu.VMEM((lons, levels, lats), F32),
            pltpu.VMEM((lons, levels, lats), BF16),
            pltpu.VMEM((lons, levels, lats), BF16),
            dma((12,)),
            dma((steps, 4)),
            dma((steps, 4)),
            dma((4,)),
            dma((4,)),
            dma((CHUNKS, 4)),
            dma((CHUNKS, 4)),
            dma((len(GROUPS) + 1, slots)),
            dma((len(GROUPS) + 1, slots)),
            dma((len(GROUPS), 4)),
            dma((len(GROUPS), 4)),
        ],
        compiler_params=pltpu.CompilerParams(collective_id=0, has_side_effects=True),
    )(
        innovations,
        courant,
        diffusivity,
        sea_bricks.reshape(levels, lats // 2),
        tile_ranks,
        jnp.swapaxes(row_factors[0], 1, 2),
        jnp.swapaxes(column_factors[0], 1, 2),
    )
    return lam, gradient


def solution(mesh):
    placed = (
        P(None, "depth", "lon", None),
        P(None, "depth", "lon", None),
        P("depth", "lon", None),
        P("depth", "lon", None),
        P("lon", None),
        P("lon", None, None, "depth"),
        P("lon", None, None, "depth"),
    )
    return jax.shard_map(
        functools.partial(per_device, mesh.shape["lon"]),
        mesh=mesh,
        in_specs=placed,
        out_specs=(P("depth", "lon", None), P("depth", "lon", None)),
        check_vma=False,
    )
```

```python
import functools

import jax
import jax.numpy as jnp
from jax import lax
from jax.experimental import pallas as pl
from jax.experimental.pallas import tpu as pltpu
from jax.sharding import PartitionSpec as P

MESH = pl.DeviceIdType.MESH
F32, BF16 = jnp.float32, jnp.bfloat16
NT = (((1,), (1,)), ((), ()))
CHUNKS = 4
EARLY = 2
GROUPS = ((0, 1), (1, 3), (3, 4))


def kernel(
    peers, inn_h, cou_h, dif_h, sea_h, ranks, u_h, v_h, lam_o, grad_o,
    inn, cou, dif, brick, sea, coef_x, coef_z, u, v, fx, fz, rx, rz,
    blk, rblk, cs_own, cs, cr_own, cr, g_own, gs, gr,
    load, face_s, face_r, rank_s, rank_r, blk_s, blk_r, co_s, co_r, g_s, g_r,
):
    levels, lons, lats = dif.shape
    slots, ranks_here = u_h.shape[0], u_h.shape[1]
    steps = inn.shape[0] - 1
    lv = levels // CHUNKS
    lon, depth = lax.axis_index("lon"), lax.axis_index("depth")
    partner = depth + 1 - 2 * lax.rem(depth, 2)
    peer = lax.rem(depth + 2, 4)

    def lon_at(shift):
        return (lax.rem(lon + shift + peers, peers), depth)

    def send(src, dst, ssem, rsem, to):
        return pltpu.make_async_remote_copy(
            src_ref=src, dst_ref=dst, send_sem=ssem, recv_sem=rsem, device_id=to, device_id_type=MESH
        )

    barrier = pltpu.get_barrier_semaphore()
    friends = [lon_at(s) for s in range(-4, 5) if s != 0] + [(lon, lax.rem(depth + i, 4)) for i in (1, 2, 3)]
    for to in friends:
        pl.semaphore_signal(barrier, inc=1, device_id=to, device_id_type=MESH)

    def fetch(src, dst, i):
        return pltpu.make_async_copy(src, dst, load.at[i])

    first = [
        fetch(sea_h, brick, 0),
        fetch(inn_h.at[4], inn.at[4], 1),
        fetch(dif_h, dif, 2),
        fetch(cou_h.at[1], cou.at[1], 3),
    ] + [fetch(cou_h.at[0, z], cou.at[0, z], 12 + z // (levels - 1)) for z in (0, levels - 1)]
    second = [
        fetch(inn_h.at[3], inn.at[3], 5),
        fetch(cou_h.at[2], cou.at[2], 6),
        fetch(cou_h.at[0, pl.ds(1, levels - 2)], cou.at[0, pl.ds(1, levels - 2)], 4),
    ]
    third = [fetch(inn_h.at[k], inn.at[k], 7 + k) for k in (2, 1, 0)]
    u_own = fetch(u_h, u.at[:, 0:ranks_here], 10)
    v_own = fetch(v_h, v.at[:, 0:ranks_here], 11)

    for c in first + second:
        c.start()

    half = slots // 2
    rank_copies = []
    for i, (src, dst) in enumerate(((u_h, u), (u_h, u), (v_h, v), (v_h, v))):
        ks = pl.ds((i % 2) * half, half)
        rank_copies.append(
            send(
                src.at[ks], dst.at[ks, ranks_here : 2 * ranks_here],
                rank_s.at[i], rank_r.at[i], (lon, partner),
            )
        )

    for c in first:
        c.wait()
    for c in third + [u_own, v_own]:
        c.start()
    bricks = lats // 2
    spread = lax.broadcasted_iota(jnp.int32, (bricks, lats), 1) // 2 == lax.broadcasted_iota(
        jnp.int32, (bricks, lats), 0
    )
    sea[...] = jnp.dot(
        brick[...].astype(F32).astype(BF16), spread.astype(F32).astype(BF16), preferred_element_type=F32
    )
    east = lons - 1
    coef_x[0] = dif[:, east, :] - 0.5 * cou[1, :, east, :]
    coef_x[1] = dif[:, 0, :] + 0.5 * cou[1, :, 0, :]
    coef_z[0] = dif[levels - 1] - 0.5 * cou[0, levels - 1]
    coef_z[1] = dif[0] + 0.5 * cou[0, 0]

    for x in (0, east):
        inn[4, :, x, :] = inn[4, :, x, :] * sea[...]
    for z in (0, levels - 1):
        mask = jnp.broadcast_to(sea[z : z + 1], (lons, lats))
        inn[4, z, 1:east] = (inn[4, z] * mask)[1:east]

    def x_faces(n):
        return [
            send(fx.at[n, i], rx.at[n, i], face_s.at[n, i], face_r.at[n, i], lon_at(1 - 2 * i))
            for i in range(2)
        ]

    def z_faces(n):
        return [
            send(
                fz.at[n, i], rz.at[n, i], face_s.at[n, 2 + i], face_r.at[n, 2 + i],
                (lon, lax.rem(depth + 5 - 2 * i, 4)),
            )
            for i in range(2)
        ]

    sends_up, sends_down = depth < 3, depth > 0

    def start_faces(n, k):
        up, down = z_faces(n)
        to_east, to_west = x_faces(n)
        fx[n, 0] = (coef_x[0] * inn[k, :, east, :]).astype(BF16)
        to_east.start()
        fx[n, 1] = (coef_x[1] * inn[k, :, 0, :]).astype(BF16)
        to_west.start()
        fz[n, 0] = coef_z[0] * inn[k, levels - 1]
        fz[n, 1] = coef_z[1] * inn[k, 0]

        @pl.when(sends_up)
        def _():
            up.start()

        @pl.when(sends_down)
        def _():
            down.start()

    def add_faces(n, k):
        up, down = z_faces(n)
        to_east, to_west = x_faces(n)
        to_east.wait_recv()
        inn[k, :, 0, :] = inn[k, :, 0, :] + sea[...] * rx[n, 0].astype(F32)
        to_west.wait_recv()
        inn[k, :, east, :] = inn[k, :, east, :] + sea[...] * rx[n, 1].astype(F32)

        @pl.when(sends_down)
        def _():
            up.wait_recv()
            inn[k, 0] = inn[k, 0] + jnp.broadcast_to(sea[0:1], (lons, lats)) * rz[n, 0]

        @pl.when(sends_up)
        def _():
            down.wait_recv()
            z = levels - 1
            inn[k, z] = inn[k, z] + jnp.broadcast_to(sea[z : z + 1], (lons, lats)) * rz[n, 1]

    row = lax.broadcasted_iota(jnp.int32, (lons, lats), 0)
    lane = lax.broadcasted_iota(jnp.int32, (lons, lats), 1)

    def sweep(k, ends, finished):
        def level(z, lower):
            a = inn[k + 1, z]
            half_a = 0.5 * a
            da = dif[z] * a
            c0, c1, c2 = (cou[i, z] * half_a for i in range(3))
            t = inn[k, z] + (a - 6.0 * da) + lower
            t = t + jnp.where(row == 0, 0.0, pltpu.roll(da - c1, 1, 0))
            t = t + jnp.where(row == lons - 1, 0.0, pltpu.roll(da + c1, lons - 1, 0))
            t = t + jnp.where(lane == 0, 0.0, pltpu.roll(da - c2, 1, 1))
            t = t + jnp.where(lane == lats - 1, 0.0, pltpu.roll(da + c2, lats - 1, 1))
            return t, da - c0, da + c0

        def masked(z):
            return jnp.broadcast_to(sea[pl.ds(z, 1)], (lons, lats))

        def body(z, carry):
            t, p = carry
            t_new, p_new, m = level(z, p)
            inn[k, z - 1] = masked(z - 1) * (t + m)
            return t_new, p_new

        t, p, _ = level(0, jnp.zeros((lons, lats), F32))
        carry, at = (t, p), 1
        for n, end in enumerate(ends):
            carry = lax.fori_loop(at, end, body, carry, unroll=8)
            finished(n)
            at = end
        carry = lax.fori_loop(at, levels - 7, body, carry, unroll=8)
        t, _ = lax.fori_loop(levels - 7, levels, body, carry, unroll=7)
        inn[k, levels - 1] = masked(levels - 1) * t

    pl.semaphore_wait(barrier, len(friends))
    start_faces(0, 4)
    rank_copies[0].start()

    def mask_level(z, _):
        inn[4, z, 1:east] = (inn[4, z] * jnp.broadcast_to(sea[pl.ds(z, 1)], (lons, lats)))[1:east]
        return 0

    lax.fori_loop(1, levels - 1, mask_level, 0, unroll=2)
    for c in second:
        c.wait()

    def spans(p):
        if p < CHUNKS - 1:
            return ((0, lv // 2 + p * lv, lv),)
        return ((0, 0, lv // 2), (lv // 2, levels - lv // 2, lv // 2))

    def block_piece(p, x):
        rows = [inn[0, z : z + size, x, :] for _, z, size in spans(p)]
        blk[p, x] = jnp.concatenate(rows, axis=0).astype(BF16)

    def early(p):
        for x in range(1, east):
            block_piece(p, x)
        pieces[p][0].start()

    def block_send(p, i):
        at = (pl.ds(1, lons - 2), pl.ds(0, 1), pl.ds(lons - 1, 1), pl.ds(0, lons))[i]
        return send(blk.at[p, at], rblk.at[p, at], blk_s.at[p, i], blk_r.at[p, i], (lon, peer))

    pieces = [[block_send(p, i) for i in ((0, 1, 2) if p < EARLY else (3,))] for p in range(CHUNKS)]

    for n in range(steps):
        k = steps - 1 - n
        if n > 0:
            third[n - 1].wait()
        if n == steps - 1:
            sweep(k, [lv // 2 + (p + 1) * lv + 1 for p in range(EARLY)], early)
        else:
            sweep(k, (), None)
        add_faces(n, k)
        if n < steps - 1:
            start_faces(n + 1, k)
            rank_copies[n + 1].start()

    for p in range(EARLY):
        for i, x in ((1, 0), (2, east)):
            block_piece(p, x)
            pieces[p][i].start()
    for p in range(EARLY, CHUNKS):
        for x in range(lons):
            block_piece(p, x)
        if p in (2, 3):
            pieces[p][0].start()

    width = 2 * ranks_here
    col = lax.broadcasted_iota(jnp.int32, (1, slots * width), 1)
    slot, r = col // width, lax.rem(col, width)
    rank = jnp.where(r < ranks_here, depth * ranks_here + r, partner * ranks_here + r - ranks_here)
    limit = jnp.zeros_like(col)
    for s in range(slots):
        limit = jnp.where(slot == s, ranks[0, s], limit)
    keep = (rank < limit).astype(F32)
    tiles = slots // 2
    tile = 2 * width

    home = slots // 2

    def coefficients(src, first_p, last_p, dst):
        rows = (last_p - first_p) * lv
        acc = jnp.zeros((rows, slots * width), F32)
        for x in range(lons):
            left = src[first_p:last_p, x].reshape(rows, lats)
            right = u[:, :, x * lats : (x + 1) * lats].reshape(slots * width, lats)
            acc = acc + lax.dot_general(left, right, NT, preferred_element_type=F32)
        acc = (acc * keep).astype(BF16)
        for i in range(tiles):
            dst[i, first_p * lv : last_p * lv] = acc[:, i * tile : (i + 1) * tile]

    def shifts(src, dst, b, first_p, last_p):
        at = pl.ds(first_p * lv, (last_p - first_p) * lv)
        return [
            send(src.at[s // 2, at], dst.at[s, at], co_s.at[b, s], co_r.at[b, s], lon_at(s - home))
            for s in range(slots)
            if s != home
        ]

    def received(src, dst, first_p, last_p):
        at = slice(first_p * lv, last_p * lv)
        low = lax.broadcasted_iota(jnp.int32, ((last_p - first_p) * lv, tile), 1) < width
        get = lambda s: src[s // 2, at] if s == home else dst[s, at]
        return [jnp.where(low, get(2 * i), get(2 * i + 1)) for i in range(tiles)]

    def sums(parts, x):
        total = None
        for i, part in enumerate(parts):
            right = v[2 * i : 2 * i + 2, :, x * lats : (x + 1) * lats].reshape(tile, lats)
            term = jnp.dot(part, right, preferred_element_type=F32)
            total = term if total is None else total + term
        return total

    own_shifts = shifts(cs_own, cr_own, len(GROUPS), 0, CHUNKS)
    group_shifts = [shifts(cs, cr, g, *GROUPS[g]) for g in range(len(GROUPS))]
    part = lons // 4

    def sum_send(g, i):
        first_p, last_p = GROUPS[g]
        at = (pl.ds(i * part, part), pl.ds(first_p * lv, (last_p - first_p) * lv))
        return send(gs.at[at], gr.at[at], g_s.at[g, i], g_r.at[g, i], (lon, peer))

    sum_sends = [[sum_send(g, i) for i in range(4)] for g in range(len(GROUPS))]

    def group_coefficients(g):
        for p in range(*GROUPS[g]):
            for copy in pieces[p]:
                copy.wait_recv()
        coefficients(rblk, *GROUPS[g], cs)
        for copy in group_shifts[g]:
            copy.start()

    def group_sums(g):
        first_p, last_p = GROUPS[g]
        for copy in group_shifts[g]:
            copy.wait_recv()
        parts = received(cs, cr, first_p, last_p)
        for i in range(4):
            for x in range(i * part, (i + 1) * part):
                gs[x, first_p * lv : last_p * lv] = sums(parts, x).astype(BF16)
            sum_sends[g][i].start()

    u_own.wait()
    rank_copies[0].wait_recv()
    rank_copies[1].wait_recv()
    coefficients(blk, 0, CHUNKS, cs_own)
    lam_o[...] = inn[0]
    for copy in own_shifts:
        copy.start()
    group_coefficients(0)
    v_own.wait()
    rank_copies[2].wait_recv()
    rank_copies[3].wait_recv()
    group_coefficients(1)
    group_sums(0)
    group_coefficients(2)
    group_sums(1)
    group_sums(2)
    for copy in own_shifts:
        copy.wait_recv()
    parts = received(cs_own, cr_own, 0, CHUNKS)
    for x in range(lons):
        g_own[x] = sums(parts, x)

    for g, (first_p, last_p) in enumerate(GROUPS):
        for i in range(4):
            sum_sends[g][i].wait_recv()
            for x in range(i * part, (i + 1) * part):
                for p in range(first_p, last_p):
                    at = slice(p * lv, (p + 1) * lv)
                    total = g_own[x, at, :] + gr[x, at].astype(F32)
                    for row, z, size in spans(p):
                        grad_o[z : z + size, x, :] = total[row : row + size]

    for n in range(steps):
        up, down = z_faces(n)
        for copy in x_faces(n):
            copy.wait_send()

        @pl.when(sends_up)
        def _():
            up.wait_send()

        @pl.when(sends_down)
        def _():
            down.wait_send()

    for copy in rank_copies:
        copy.wait_send()
    for copies in pieces + sum_sends + group_shifts + [own_shifts]:
        for copy in copies:
            copy.wait_send()


def per_device(
    peers, innovations, courant, diffusivity, sea_bricks, tile_ranks, row_factors, column_factors
):
    levels, lons, lats = diffusivity.shape
    slots, cols, here = row_factors.shape[1:]
    steps = innovations.shape[0] - 1
    lv = levels // CHUNKS
    dma = pltpu.SemaphoreType.DMA
    anywhere = pl.BlockSpec(memory_space=pl.ANY)
    lam, gradient = pl.pallas_call(
        functools.partial(kernel, peers),
        out_shape=(pltpu.VMEM(diffusivity.shape, F32),) * 2,
        in_specs=[anywhere] * 4 + [pl.BlockSpec(memory_space=pltpu.SMEM)] + [anywhere] * 2,
        out_specs=(pl.BlockSpec(memory_space=pltpu.VMEM),) * 2,
        scratch_shapes=[
            pltpu.VMEM(innovations.shape, F32),
            pltpu.VMEM(courant.shape, F32),
            pltpu.VMEM(diffusivity.shape, F32),
            pltpu.VMEM((levels, lats // 2), jnp.int32),
            pltpu.VMEM((levels, lats), F32),
            pltpu.VMEM((2, levels, lats), F32),
            pltpu.VMEM((2, lons, lats), F32),
            pltpu.VMEM((slots, 2 * here, cols), BF16),
            pltpu.VMEM((slots, 2 * here, cols), BF16),
            pltpu.VMEM((steps, 2, levels, lats), BF16),
            pltpu.VMEM((steps, 2, lons, lats), F32),
            pltpu.VMEM((steps, 2, levels, lats), BF16),
            pltpu.VMEM((steps, 2, lons, lats), F32),
            pltpu.VMEM((CHUNKS, lons, lv, lats), BF16),
            pltpu.VMEM((CHUNKS, lons, lv, lats), BF16),
            pltpu.VMEM((slots // 2, levels, 4 * here), BF16),
            pltpu.VMEM((slots // 2, levels, 4 * here), BF16),
            pltpu.VMEM((slots, levels, 4 * here), BF16),
            pltpu.VMEM((slots, levels, 4 * here), BF16),
            pltpu.VMEM((lons, levels, lats), F32),
            pltpu.VMEM((lons, levels, lats), BF16),
            pltpu.VMEM((lons, levels, lats), BF16),
            dma((14,)),
            dma((steps, 4)),
            dma((steps, 4)),
            dma((4,)),
            dma((4,)),
            dma((CHUNKS, 4)),
            dma((CHUNKS, 4)),
            dma((len(GROUPS) + 1, slots)),
            dma((len(GROUPS) + 1, slots)),
            dma((len(GROUPS), 4)),
            dma((len(GROUPS), 4)),
        ],
        compiler_params=pltpu.CompilerParams(collective_id=0, has_side_effects=True),
    )(
        innovations,
        courant,
        diffusivity,
        sea_bricks.reshape(levels, lats // 2),
        tile_ranks,
        jnp.swapaxes(row_factors[0], 1, 2),
        jnp.swapaxes(column_factors[0], 1, 2),
    )
    return lam, gradient


def solution(mesh):
    placed = (
        P(None, "depth", "lon", None),
        P(None, "depth", "lon", None),
        P("depth", "lon", None),
        P("depth", "lon", None),
        P("lon", None),
        P("lon", None, None, "depth"),
        P("lon", None, None, "depth"),
    )
    return jax.shard_map(
        functools.partial(per_device, mesh.shape["lon"]),
        mesh=mesh,
        in_specs=placed,
        out_specs=(P("depth", "lon", None), P("depth", "lon", None)),
        check_vma=False,
    )
```

```python
import functools

import jax
import jax.numpy as jnp
from jax import lax
from jax.experimental import pallas as pl
from jax.experimental.pallas import tpu as pltpu
from jax.sharding import PartitionSpec as P

MESH = pl.DeviceIdType.MESH
F32, BF16 = jnp.float32, jnp.bfloat16
NT = (((1,), (1,)), ((), ()))
CHUNKS = 4
EARLY = 2
GROUPS = ((0, 1), (1, 3), (3, 4))


def kernel(
    peers, inn_h, cou_h, dif_h, sea_h, ranks, u_h, v_h, lam_o, grad_o,
    inn, cou, dif, brick, sea, coef_x, coef_z, u, v, fx, fz, rx, rz,
    blk, rblk, cs_own, cs, cr_own, cr, g_own, gs, gr,
    load, face_s, face_r, rank_s, rank_r, blk_s, blk_r, co_s, co_r, g_s, g_r,
):
    levels, lons, lats = dif.shape
    slots, ranks_here = u_h.shape[0], u_h.shape[1]
    steps = inn.shape[0] - 1
    lv = levels // CHUNKS
    lon, depth = lax.axis_index("lon"), lax.axis_index("depth")
    partner = depth + 1 - 2 * lax.rem(depth, 2)
    peer = lax.rem(depth + 2, 4)

    def lon_at(shift):
        return (lax.rem(lon + shift + peers, peers), depth)

    def send(src, dst, ssem, rsem, to):
        return pltpu.make_async_remote_copy(
            src_ref=src, dst_ref=dst, send_sem=ssem, recv_sem=rsem, device_id=to, device_id_type=MESH
        )

    barrier = pltpu.get_barrier_semaphore()
    friends = [lon_at(s) for s in range(-4, 5) if s != 0] + [(lon, lax.rem(depth + i, 4)) for i in (1, 2, 3)]
    for to in friends:
        pl.semaphore_signal(barrier, inc=1, device_id=to, device_id_type=MESH)

    def fetch(src, dst, i):
        return pltpu.make_async_copy(src, dst, load.at[i])

    first = [
        fetch(sea_h, brick, 0),
        fetch(inn_h.at[4], inn.at[4], 1),
        fetch(dif_h, dif, 2),
        fetch(cou_h.at[1], cou.at[1], 3),
    ] + [fetch(cou_h.at[0, z], cou.at[0, z], 12 + z // (levels - 1)) for z in (0, levels - 1)]
    second = [
        fetch(inn_h.at[3], inn.at[3], 5),
        fetch(cou_h.at[2], cou.at[2], 6),
        fetch(cou_h.at[0, pl.ds(1, levels - 2)], cou.at[0, pl.ds(1, levels - 2)], 4),
    ]
    third = [fetch(inn_h.at[k], inn.at[k], 7 + k) for k in (2, 1, 0)]
    u_own = fetch(u_h, u.at[:, 0:ranks_here], 10)
    v_own = fetch(v_h, v.at[:, 0:ranks_here], 11)

    for c in first + second:
        c.start()

    half = slots // 2
    rank_copies = []
    for i, (src, dst) in enumerate(((u_h, u), (u_h, u), (v_h, v), (v_h, v))):
        ks = pl.ds((i % 2) * half, half)
        rank_copies.append(
            send(
                src.at[ks], dst.at[ks, ranks_here : 2 * ranks_here],
                rank_s.at[i], rank_r.at[i], (lon, partner),
            )
        )

    for c in first:
        c.wait()
    for c in third + [u_own, v_own]:
        c.start()
    bricks = lats // 2
    spread = lax.broadcasted_iota(jnp.int32, (bricks, lats), 1) // 2 == lax.broadcasted_iota(
        jnp.int32, (bricks, lats), 0
    )
    sea[...] = jnp.dot(
        brick[...].astype(F32).astype(BF16), spread.astype(F32).astype(BF16), preferred_element_type=F32
    )
    east = lons - 1
    coef_x[0] = dif[:, east, :] - 0.5 * cou[1, :, east, :]
    coef_x[1] = dif[:, 0, :] + 0.5 * cou[1, :, 0, :]
    coef_z[0] = dif[levels - 1] - 0.5 * cou[0, levels - 1]
    coef_z[1] = dif[0] + 0.5 * cou[0, 0]

    for x in (0, east):
        inn[4, :, x, :] = inn[4, :, x, :] * sea[...]
    for z in (0, levels - 1):
        mask = jnp.broadcast_to(sea[z : z + 1], (lons, lats))
        inn[4, z, 1:east] = (inn[4, z] * mask)[1:east]

    def x_faces(n):
        return [
            send(fx.at[n, i], rx.at[n, i], face_s.at[n, i], face_r.at[n, i], lon_at(1 - 2 * i))
            for i in range(2)
        ]

    def z_faces(n):
        return [
            send(
                fz.at[n, i], rz.at[n, i], face_s.at[n, 2 + i], face_r.at[n, 2 + i],
                (lon, lax.rem(depth + 5 - 2 * i, 4)),
            )
            for i in range(2)
        ]

    sends_up, sends_down = depth < 3, depth > 0

    def start_faces(n, k):
        up, down = z_faces(n)
        to_east, to_west = x_faces(n)
        fx[n, 0] = (coef_x[0] * inn[k, :, east, :]).astype(BF16)
        to_east.start()
        fx[n, 1] = (coef_x[1] * inn[k, :, 0, :]).astype(BF16)
        to_west.start()
        fz[n, 0] = coef_z[0] * inn[k, levels - 1]
        fz[n, 1] = coef_z[1] * inn[k, 0]

        @pl.when(sends_up)
        def _():
            up.start()

        @pl.when(sends_down)
        def _():
            down.start()

    def add_faces(n, k):
        up, down = z_faces(n)
        to_east, to_west = x_faces(n)
        to_east.wait_recv()
        inn[k, :, 0, :] = inn[k, :, 0, :] + sea[...] * rx[n, 0].astype(F32)
        to_west.wait_recv()
        inn[k, :, east, :] = inn[k, :, east, :] + sea[...] * rx[n, 1].astype(F32)

        @pl.when(sends_down)
        def _():
            up.wait_recv()
            inn[k, 0] = inn[k, 0] + jnp.broadcast_to(sea[0:1], (lons, lats)) * rz[n, 0]

        @pl.when(sends_up)
        def _():
            down.wait_recv()
            z = levels - 1
            inn[k, z] = inn[k, z] + jnp.broadcast_to(sea[z : z + 1], (lons, lats)) * rz[n, 1]

    row = lax.broadcasted_iota(jnp.int32, (lons, lats), 0)
    lane = lax.broadcasted_iota(jnp.int32, (lons, 128), 1)

    def sweep(k, ends, finished):
        def level(z, lower):
            a = inn[k + 1, z]
            half_a = 0.5 * a
            da = dif[z] * a
            c0, c1, c2 = (cou[i, z] * half_a for i in range(3))
            t = inn[k, z] + (a - 6.0 * da) + lower
            t = t + jnp.where(row == 0, 0.0, pltpu.roll(da - c1, 1, 0))
            t = t + jnp.where(row == lons - 1, 0.0, pltpu.roll(da + c1, lons - 1, 0))
            p, m = da - c2, da + c2
            p0, p1 = (pltpu.roll(p[:, i * 128 : (i + 1) * 128], 1, 1) for i in range(2))
            m0, m1 = (pltpu.roll(m[:, i * 128 : (i + 1) * 128], 127, 1) for i in range(2))
            left = jnp.where(lane == 0, 0.0, p0) + jnp.where(lane == 127, m1, m0)
            right = jnp.where(lane == 0, p0, p1) + jnp.where(lane == 127, 0.0, m1)
            t = t + jnp.concatenate([left, right], axis=1)
            return t, da - c0, da + c0

        def masked(z):
            return jnp.broadcast_to(sea[pl.ds(z, 1)], (lons, lats))

        def body(z, carry):
            t, p = carry
            t_new, p_new, m = level(z, p)
            inn[k, z - 1] = masked(z - 1) * (t + m)
            return t_new, p_new

        t, p, _ = level(0, jnp.zeros((lons, lats), F32))
        carry, at = (t, p), 1
        for n, end in enumerate(ends):
            carry = lax.fori_loop(at, end, body, carry, unroll=8)
            finished(n)
            at = end
        carry = lax.fori_loop(at, levels - 7, body, carry, unroll=8)
        t, _ = lax.fori_loop(levels - 7, levels, body, carry, unroll=7)
        inn[k, levels - 1] = masked(levels - 1) * t

    pl.semaphore_wait(barrier, len(friends))
    start_faces(0, 4)
    rank_copies[0].start()
    rank_copies[1].start()

    def mask_level(z, _):
        inn[4, z, 1:east] = (inn[4, z] * jnp.broadcast_to(sea[pl.ds(z, 1)], (lons, lats)))[1:east]
        return 0

    lax.fori_loop(1, levels - 1, mask_level, 0, unroll=2)
    for c in second:
        c.wait()

    def spans(p):
        if p < CHUNKS - 1:
            return ((0, lv // 2 + p * lv, lv),)
        return ((0, 0, lv // 2), (lv // 2, levels - lv // 2, lv // 2))

    def block_piece(p, x):
        rows = [inn[0, z : z + size, x, :] for _, z, size in spans(p)]
        blk[p, x] = jnp.concatenate(rows, axis=0).astype(BF16)

    def early(p):
        for x in range(1, east):
            block_piece(p, x)
        pieces[p][0].start()

    def block_send(p, i):
        at = (pl.ds(1, lons - 2), pl.ds(0, 1), pl.ds(lons - 1, 1), pl.ds(0, lons))[i]
        return send(blk.at[p, at], rblk.at[p, at], blk_s.at[p, i], blk_r.at[p, i], (lon, peer))

    pieces = [[block_send(p, i) for i in ((0, 1, 2) if p < EARLY else (3,))] for p in range(CHUNKS)]

    for n in range(steps):
        k = steps - 1 - n
        if n > 0:
            third[n - 1].wait()
        if n == steps - 1:
            sweep(k, [lv // 2 + (p + 1) * lv + 1 for p in range(EARLY)], early)
        else:
            sweep(k, (), None)
        add_faces(n, k)
        if n < steps - 1:
            start_faces(n + 1, k)
            if n + 2 < len(rank_copies):
                rank_copies[n + 2].start()

    for p in range(EARLY):
        for i, x in ((1, 0), (2, east)):
            block_piece(p, x)
            pieces[p][i].start()
    for p in range(EARLY, CHUNKS):
        for x in range(lons):
            block_piece(p, x)
        if p in (2, 3):
            pieces[p][0].start()

    width = 2 * ranks_here
    col = lax.broadcasted_iota(jnp.int32, (1, slots * width), 1)
    slot, r = col // width, lax.rem(col, width)
    rank = jnp.where(r < ranks_here, depth * ranks_here + r, partner * ranks_here + r - ranks_here)
    limit = jnp.zeros_like(col)
    for s in range(slots):
        limit = jnp.where(slot == s, ranks[0, s], limit)
    keep = (rank < limit).astype(F32)
    tiles = slots // 2
    tile = 2 * width

    home = slots // 2

    def coefficients(src, first_p, last_p, dst):
        rows = (last_p - first_p) * lv
        acc = jnp.zeros((rows, slots * width), F32)
        for x in range(lons):
            left = src[first_p:last_p, x].reshape(rows, lats)
            right = u[:, :, x * lats : (x + 1) * lats].reshape(slots * width, lats)
            acc = acc + lax.dot_general(left, right, NT, preferred_element_type=F32)
        acc = (acc * keep).astype(BF16)
        for i in range(tiles):
            dst[i, first_p * lv : last_p * lv] = acc[:, i * tile : (i + 1) * tile]

    def shifts(src, dst, b, first_p, last_p):
        at = pl.ds(first_p * lv, (last_p - first_p) * lv)
        return [
            send(src.at[s // 2, at], dst.at[s, at], co_s.at[b, s], co_r.at[b, s], lon_at(s - home))
            for s in range(slots)
            if s != home
        ]

    def received(src, dst, first_p, last_p):
        at = slice(first_p * lv, last_p * lv)
        low = lax.broadcasted_iota(jnp.int32, ((last_p - first_p) * lv, tile), 1) < width
        get = lambda s: src[s // 2, at] if s == home else dst[s, at]
        return [jnp.where(low, get(2 * i), get(2 * i + 1)) for i in range(tiles)]

    def sums(parts, x):
        total = None
        for i, part in enumerate(parts):
            right = v[2 * i : 2 * i + 2, :, x * lats : (x + 1) * lats].reshape(tile, lats)
            term = jnp.dot(part, right, preferred_element_type=F32)
            total = term if total is None else total + term
        return total

    own_shifts = shifts(cs_own, cr_own, len(GROUPS), 0, CHUNKS)
    group_shifts = [shifts(cs, cr, g, *GROUPS[g]) for g in range(len(GROUPS))]
    part = lons // 4

    def sum_send(g, i):
        first_p, last_p = GROUPS[g]
        at = (pl.ds(i * part, part), pl.ds(first_p * lv, (last_p - first_p) * lv))
        return send(gs.at[at], gr.at[at], g_s.at[g, i], g_r.at[g, i], (lon, peer))

    sum_sends = [[sum_send(g, i) for i in range(4)] for g in range(len(GROUPS))]

    def group_coefficients(g):
        for p in range(*GROUPS[g]):
            for copy in pieces[p]:
                copy.wait_recv()
        coefficients(rblk, *GROUPS[g], cs)
        for copy in group_shifts[g]:
            copy.start()

    def group_sums(g):
        first_p, last_p = GROUPS[g]
        for copy in group_shifts[g]:
            copy.wait_recv()
        parts = received(cs, cr, first_p, last_p)
        for i in range(4):
            for x in range(i * part, (i + 1) * part):
                gs[x, first_p * lv : last_p * lv] = sums(parts, x).astype(BF16)
            sum_sends[g][i].start()

    u_own.wait()
    rank_copies[0].wait_recv()
    rank_copies[1].wait_recv()
    coefficients(blk, 0, CHUNKS, cs_own)
    lam_o[...] = inn[0]
    for copy in own_shifts:
        copy.start()
    group_coefficients(0)
    v_own.wait()
    rank_copies[2].wait_recv()
    rank_copies[3].wait_recv()
    group_coefficients(1)
    group_sums(0)
    group_coefficients(2)
    group_sums(1)
    group_sums(2)
    for copy in own_shifts:
        copy.wait_recv()
    parts = received(cs_own, cr_own, 0, CHUNKS)
    for x in range(lons):
        g_own[x] = sums(parts, x)

    for g, (first_p, last_p) in enumerate(GROUPS):
        for i in range(4):
            sum_sends[g][i].wait_recv()
            for x in range(i * part, (i + 1) * part):
                for p in range(first_p, last_p):
                    at = slice(p * lv, (p + 1) * lv)
                    total = g_own[x, at, :] + gr[x, at].astype(F32)
                    for row, z, size in spans(p):
                        grad_o[z : z + size, x, :] = total[row : row + size]

    for n in range(steps):
        up, down = z_faces(n)
        for copy in x_faces(n):
            copy.wait_send()

        @pl.when(sends_up)
        def _():
            up.wait_send()

        @pl.when(sends_down)
        def _():
            down.wait_send()

    for copy in rank_copies:
        copy.wait_send()
    for copies in pieces + sum_sends + group_shifts + [own_shifts]:
        for copy in copies:
            copy.wait_send()


def per_device(
    peers, innovations, courant, diffusivity, sea_bricks, tile_ranks, row_factors, column_factors
):
    levels, lons, lats = diffusivity.shape
    slots, cols, here = row_factors.shape[1:]
    steps = innovations.shape[0] - 1
    lv = levels // CHUNKS
    dma = pltpu.SemaphoreType.DMA
    anywhere = pl.BlockSpec(memory_space=pl.ANY)
    lam, gradient = pl.pallas_call(
        functools.partial(kernel, peers),
        out_shape=(pltpu.VMEM(diffusivity.shape, F32),) * 2,
        in_specs=[anywhere] * 4 + [pl.BlockSpec(memory_space=pltpu.SMEM)] + [anywhere] * 2,
        out_specs=(pl.BlockSpec(memory_space=pltpu.VMEM),) * 2,
        scratch_shapes=[
            pltpu.VMEM(innovations.shape, F32),
            pltpu.VMEM(courant.shape, F32),
            pltpu.VMEM(diffusivity.shape, F32),
            pltpu.VMEM((levels, lats // 2), jnp.int32),
            pltpu.VMEM((levels, lats), F32),
            pltpu.VMEM((2, levels, lats), F32),
            pltpu.VMEM((2, lons, lats), F32),
            pltpu.VMEM((slots, 2 * here, cols), BF16),
            pltpu.VMEM((slots, 2 * here, cols), BF16),
            pltpu.VMEM((steps, 2, levels, lats), BF16),
            pltpu.VMEM((steps, 2, lons, lats), F32),
            pltpu.VMEM((steps, 2, levels, lats), BF16),
            pltpu.VMEM((steps, 2, lons, lats), F32),
            pltpu.VMEM((CHUNKS, lons, lv, lats), BF16),
            pltpu.VMEM((CHUNKS, lons, lv, lats), BF16),
            pltpu.VMEM((slots // 2, levels, 4 * here), BF16),
            pltpu.VMEM((slots // 2, levels, 4 * here), BF16),
            pltpu.VMEM((slots, levels, 4 * here), BF16),
            pltpu.VMEM((slots, levels, 4 * here), BF16),
            pltpu.VMEM((lons, levels, lats), F32),
            pltpu.VMEM((lons, levels, lats), BF16),
            pltpu.VMEM((lons, levels, lats), BF16),
            dma((14,)),
            dma((steps, 4)),
            dma((steps, 4)),
            dma((4,)),
            dma((4,)),
            dma((CHUNKS, 4)),
            dma((CHUNKS, 4)),
            dma((len(GROUPS) + 1, slots)),
            dma((len(GROUPS) + 1, slots)),
            dma((len(GROUPS), 4)),
            dma((len(GROUPS), 4)),
        ],
        compiler_params=pltpu.CompilerParams(collective_id=0, has_side_effects=True),
    )(
        innovations,
        courant,
        diffusivity,
        sea_bricks.reshape(levels, lats // 2),
        tile_ranks,
        jnp.swapaxes(row_factors[0], 1, 2),
        jnp.swapaxes(column_factors[0], 1, 2),
    )
    return lam, gradient


def solution(mesh):
    placed = (
        P(None, "depth", "lon", None),
        P(None, "depth", "lon", None),
        P("depth", "lon", None),
        P("depth", "lon", None),
        P("lon", None),
        P("lon", None, None, "depth"),
        P("lon", None, None, "depth"),
    )
    return jax.shard_map(
        functools.partial(per_device, mesh.shape["lon"]),
        mesh=mesh,
        in_specs=placed,
        out_specs=(P("depth", "lon", None), P("depth", "lon", None)),
        check_vma=False,
    )
```
